768 devices in a mesh: wide: 32 (over x, y_lo, core), pair: 12 (over z), sub: 2 (over y_hi).
Axes of the slice: x: 4, y: 8 (y_hi: 2, y_lo: 4; y = y_hi * 4 + y_lo), z: 12, core: 2. Of those that a mesh axis runs over, the one named last changes fastest.
Arguments:
- orbitals: bfloat16 [6, 64, 160, 160], P(None, ('wide', 'sub')), may hold values from -0.5 to 0.5
- couplings: bfloat16 [24, 160, 160], P('pair'), may hold values from -6 to 6
- blocks: int32 [24, 2], P('pair'), may hold values from 0 to 5, as said below
- partner: int32 [24], P('pair'), may hold values from 0 to 23, as said below
Outputs:
- self_energy: bfloat16 [24, 64, 160, 160], P('pair', ('wide', 'sub'))
The draws below stay inside these ranges and needn't reach their ends.
Inputs may be any that keep to these rules, and one draw needn't show every extreme that they name: blocks[partner[b]] is blocks[b] with its two entries swapped, and the two entries of a row differ. partner is an involution without fixed points; the partner of a block lies among the 2 blocks of the index of pair that is half the pair axis away.
All inputs are finite; a program needn't handle non-finite values.
Results may differ from the reference program's by a relative error of at most 0.014.
Values may be sent and summed in bfloat16 or wider, within the bound.
No kernel may reach another device: no remote copies, remote signals or barrier semaphores. Data moves between devices by JAX's collectives and lax.ppermute only.
A program may use at most 32 MiB of HBM per device.

```python
import jax
import jax.numpy as jnp
from jax import lax

ORDER = 160
BLK_DEV = 2
NSITE = 6
NE = 64
NBLK = 24
N_PAIR = 12


def mirror_table(key):
    base = jax.random.fold_in(key, 4111)
    subkey_one, subkey_two, subkey_three = jax.random.split(base, 3)
    half_axis = N_PAIR // 2
    first = jax.random.randint(subkey_one, (half_axis, BLK_DEV), 0, NSITE)
    offset = jax.random.randint(subkey_two, (half_axis, BLK_DEV), 1, NSITE)
    first = first.at[0, 0].set(0)
    offset = offset.at[0, 0].set(NSITE - 1)
    second = (first + offset) % NSITE
    scores = jax.random.randint(subkey_three, (half_axis, BLK_DEV), 0, 4096) * BLK_DEV + jnp.arange(BLK_DEV)[None, :]
    ordering = jnp.argsort(scores, axis=1).astype(jnp.int32)
    inverse = jnp.argsort(ordering, axis=1).astype(jnp.int32)
    row_index = jnp.arange(half_axis, dtype=jnp.int32)[:, None]
    low_sites = jnp.stack([first, second], -1)
    high_sites = jnp.take_along_axis(jnp.stack([second, first], -1), inverse[:, :, None], axis=1)
    low_partner = (row_index + half_axis) * BLK_DEV + ordering
    high_partner = row_index * BLK_DEV + inverse
    sites_all = jnp.concatenate([low_sites.reshape(-1, 2), high_sites.reshape(-1, 2)], 0).astype(jnp.int32)
    partner_all = jnp.concatenate([low_partner.reshape(-1), high_partner.reshape(-1)], 0).astype(jnp.int32)
    return (sites_all, partner_all)


def draw_blocks(key, part):
    return mirror_table(key)[0]


def draw_partner(key, part):
    return mirror_table(key)[1]


def shard_levels(key, extent, pieces, low, top_value):
    loudness = 1.0
    for axis_at, parts in pieces:
        steps = jax.random.uniform(jax.random.fold_in(jax.random.fold_in(key, 6), axis_at), (parts,), jnp.float32, low / len(pieces), top_value / len(pieces))
        loudness = loudness * jnp.repeat(jnp.exp(steps), extent[axis_at] // parts).reshape((-1,) + (1,) * (len(extent) - 1 - axis_at))
    return loudness


def centred(stream_key, dims, deviation, reach, cuts=(), held_as=jnp.bfloat16):
    entries = deviation * jax.random.normal(stream_key, dims, jnp.float32)
    if cuts:
        entries = entries * shard_levels(stream_key, dims, cuts, -0.22, 0.18)
    return jnp.clip(entries, -reach, reach).astype(held_as)


def setup_inputs(seed: int = 0) -> dict:
    streams_of = jax.random.split(jax.random.key(seed), 5)
    return {
        "orbitals": centred(streams_of[0], (NSITE, NE, ORDER, ORDER), ORDER ** -0.5, 0.5, ((1, 64),)),
        "couplings": centred(streams_of[1], (NBLK, ORDER, ORDER), 1.0, 6.0, ((0, 12),)),
        "blocks": draw_blocks(jax.random.fold_in(streams_of[4], 71), 0),
        "partner": draw_partner(jax.random.fold_in(streams_of[4], 71), 0),
    }


def triple_product(left_side, middle, right_side):
    inner_prod = jnp.einsum('emn,enk->emk', left_side.astype(jnp.float32), middle.astype(jnp.float32)).astype(jnp.bfloat16)
    return jnp.einsum('emk,enk->emn', inner_prod.astype(jnp.float32), right_side.astype(jnp.float32)).astype(jnp.bfloat16)


def reference(orbitals, couplings, blocks, partner):
    def forward_block(blk_index):
        middle = jnp.broadcast_to(couplings[blk_index], (NE, ORDER, ORDER))
        return triple_product(orbitals[blocks[blk_index, 0]], middle, orbitals[blocks[blk_index, 1]])

    direct = lax.map(forward_block, jnp.arange(NBLK, dtype=jnp.int32))

    def screen_block(blk_index):
        first = direct[blk_index].astype(jnp.float32)
        second = jnp.swapaxes(direct[partner[blk_index]], 1, 2).astype(jnp.float32)
        spectra = jnp.fft.rfft(first, n=2 * NE, axis=0) * jnp.fft.rfft(second, n=2 * NE, axis=0)
        convolved = jnp.fft.irfft(spectra, n=2 * NE, axis=0)[:NE] * (NE ** -0.5)
        polar = convolved.astype(jnp.bfloat16)
        return triple_product(orbitals[blocks[blk_index, 0]], polar, orbitals[blocks[blk_index, 1]])

    return lax.map(screen_block, jnp.arange(NBLK, dtype=jnp.int32))
```

```python
import functools

import jax
import jax.numpy as jnp
from jax import lax
from jax.experimental import pallas as pl
from jax.experimental.pallas import tpu as pltpu
from jax.sharding import PartitionSpec as P

LANES = 128
ROWS = 8
VMEM = pl.BlockSpec(memory_space=pltpu.VMEM)
SMEM = pl.BlockSpec(memory_space=pltpu.SMEM)


def matmul(left, right):
    return jnp.dot(left, right, preferred_element_type=jnp.float32)


def matmul_t(left, right):
    return lax.dot_general(
        left, right, (((1,), (1,)), ((), ())), preferred_element_type=jnp.float32
    )


def pack(first, second):
    half = first.shape[0] // 2
    rest = jnp.concatenate(
        [
            first[:half, LANES:],
            first[half:, LANES:],
            second[:half, LANES:],
            second[half:, LANES:],
        ],
        axis=1,
    )
    return jnp.concatenate([first[:, :LANES], second[:, :LANES], rest], axis=0)


def direct_kernel(blocks, orbitals, couplings, out):
    results = []
    for b in range(2):
        left = orbitals[blocks[b, 0]]
        right = orbitals[blocks[b, 1]]
        inner = matmul(left, couplings[b]).astype(jnp.bfloat16)
        results.append(matmul_t(inner, right))
    out[...] = pack(*results).astype(jnp.bfloat16)


def mirror_kernel(blocks, partner, orbitals, shifted, direct, out):
    results = []
    for b in range(2):
        left = orbitals[blocks[b, 0]]
        right = orbitals[blocks[b, 1]]
        across = matmul(right, shifted[lax.rem(partner[b], 2)]).astype(jnp.bfloat16)
        results.append(matmul_t(left, across))
    mirror = pack(*results)
    used = direct.shape[0] // ROWS
    both = jnp.concatenate(
        [
            direct[...].astype(jnp.float32).reshape(used, ROWS, LANES),
            mirror.reshape(used, ROWS, LANES),
        ],
        axis=1,
    )
    out[:used] = both.astype(jnp.bfloat16)
    out[used:] = jnp.zeros((out.shape[0] - used, 2 * ROWS, LANES), jnp.bfloat16)


def convolve_kernel(tile, incoming, out, first, second):
    count = incoming.shape[0]
    both = incoming[...].astype(jnp.float32)
    first[...] = both[:, :ROWS]
    second[...] = both[:, ROWS:]
    scale = count ** (-0.5)
    for e0 in range(0, count, tile):
        totals = [None] * tile
        for t0 in range(0, e0 + tile, tile):
            lhs = [first[t0 + k] for k in range(tile)]
            base = e0 - t0 - tile + 1
            rhs = [
                second[base + k] if base + k >= 0 else None for k in range(2 * tile - 1)
            ]
            for de in range(tile):
                for dt in range(tile):
                    other = rhs[de - dt + tile - 1]
                    if other is None:
                        continue
                    term = lhs[dt] * other
                    totals[de] = term if totals[de] is None else totals[de] + term
        for de in range(0, tile, 2):
            pair = jnp.concatenate([totals[de], totals[de + 1]], axis=0) * scale
            out[pl.ds((e0 + de) * ROWS, 2 * ROWS), :] = pair.astype(jnp.bfloat16)


def screen_kernel(blocks, orbitals, packed, out):
    order = out.shape[1]
    half = order // 2
    rest = packed[2 * order : 2 * order + half, :]
    width = order - LANES
    for b in range(2):
        left = orbitals[blocks[b, 0]]
        right = orbitals[blocks[b, 1]]
        at = 2 * b * width
        tail = jnp.concatenate(
            [rest[:, at : at + width], rest[:, at + width : at + 2 * width]], axis=0
        )
        polar = jnp.concatenate([packed[b * order : (b + 1) * order, :], tail], axis=1)
        screened = matmul(left, polar).astype(jnp.bfloat16)
        out[b] = matmul_t(screened, right).astype(jnp.bfloat16)


def per_device(orbitals, couplings, blocks, partner):
    axes = ("wide", "sub")
    energies = lax.axis_size("wide") * lax.axis_size("sub")
    pairs = lax.axis_size("pair")
    order = couplings.shape[1]
    packed_rows = 2 * order * order // LANES
    shifted = lax.ppermute(
        couplings, "pair", [(i, (i + pairs // 2) % pairs) for i in range(pairs)]
    )
    sites = orbitals.reshape(orbitals.shape[0], order, order)
    direct = pl.pallas_call(
        direct_kernel,
        out_shape=jax.ShapeDtypeStruct((packed_rows, LANES), jnp.bfloat16),
        in_specs=[SMEM, VMEM, VMEM],
        out_specs=VMEM,
        name="direct",
    )(blocks, sites, couplings)
    outgoing = pl.pallas_call(
        mirror_kernel,
        out_shape=jax.ShapeDtypeStruct((energies, 2 * ROWS, LANES), jnp.bfloat16),
        in_specs=[SMEM, SMEM, VMEM, VMEM, VMEM],
        out_specs=VMEM,
        name="mirror",
    )(blocks, partner, sites, shifted, direct)
    incoming = lax.all_to_all(outgoing, axes, split_axis=0, concat_axis=0, tiled=True)
    polar = pl.pallas_call(
        functools.partial(convolve_kernel, 8),
        out_shape=jax.ShapeDtypeStruct((energies * ROWS, LANES), jnp.bfloat16),
        in_specs=[VMEM],
        out_specs=VMEM,
        scratch_shapes=[pltpu.VMEM((energies, ROWS, LANES), jnp.float32)] * 2,
        name="convolve",
    )(incoming)
    returned = lax.all_to_all(
        polar.reshape(energies, ROWS, LANES), axes, split_axis=0, concat_axis=0, tiled=True
    )
    result = pl.pallas_call(
        screen_kernel,
        out_shape=jax.ShapeDtypeStruct(couplings.shape, jnp.bfloat16),
        in_specs=[SMEM, VMEM, VMEM],
        out_specs=VMEM,
        name="screen",
    )(blocks, sites, returned.reshape(energies * ROWS, LANES))
    return result.reshape(couplings.shape[0], 1, order, order)


def solution(mesh):
    placed = (
        P(None, ("wide", "sub"), None, None),
        P("pair", None, None),
        P("pair", None),
        P("pair"),
    )
    return jax.shard_map(
        per_device,
        mesh=mesh,
        in_specs=placed,
        out_specs=P("pair", ("wide", "sub"), None, None),
        check_vma=False,
    )
```

```python
import functools

import jax
import jax.numpy as jnp
from jax import lax
from jax.experimental import pallas as pl
from jax.experimental.pallas import tpu as pltpu
from jax.sharding import PartitionSpec as P

LANES = 128
ROWS = 8
VMEM = pl.BlockSpec(memory_space=pltpu.VMEM)
SMEM = pl.BlockSpec(memory_space=pltpu.SMEM)


def matmul(left, right):
    return jnp.dot(left, right, preferred_element_type=jnp.float32)


def matmul_t(left, right):
    return lax.dot_general(
        left, right, (((1,), (1,)), ((), ())), preferred_element_type=jnp.float32
    )


def pack(first, second):
    half = first.shape[0] // 2
    rest = jnp.concatenate(
        [
            first[:half, LANES:],
            first[half:, LANES:],
            second[:half, LANES:],
            second[half:, LANES:],
        ],
        axis=1,
    )
    return jnp.concatenate([first[:, :LANES], second[:, :LANES], rest], axis=0)


def direct_kernel(blocks, orbitals, couplings, out):
    results = []
    for b in range(2):
        left = orbitals[blocks[b, 0]]
        right = orbitals[blocks[b, 1]]
        inner = matmul(left, couplings[b]).astype(jnp.bfloat16)
        results.append(matmul_t(inner, right))
    out[...] = pack(*results).astype(jnp.bfloat16)


def mirror_kernel(blocks, partner, orbitals, shifted, direct, out):
    results = []
    for b in range(2):
        left = orbitals[blocks[b, 0]]
        right = orbitals[blocks[b, 1]]
        across = matmul(right, shifted[lax.rem(partner[b], 2)]).astype(jnp.bfloat16)
        results.append(matmul_t(left, across))
    mirror = pack(*results)
    used = direct.shape[0] // ROWS
    both = jnp.concatenate(
        [
            direct[...].astype(jnp.float32).reshape(used, ROWS, LANES),
            mirror.reshape(used, ROWS, LANES),
        ],
        axis=1,
    )
    out[:used] = both.astype(jnp.bfloat16)
    out[used:] = jnp.zeros((out.shape[0] - used, 2 * ROWS, LANES), jnp.bfloat16)


def convolve_kernel(tile, incoming, out, first, second):
    count = incoming.shape[0]
    both = incoming[...].astype(jnp.float32)
    first[...] = both[:, :ROWS]
    second[...] = both[:, ROWS:]
    scale = count ** (-0.5)
    for e0 in range(0, count, tile):
        totals = [None] * tile
        for t0 in range(0, e0 + tile, tile):
            lhs = [first[t0 + k] for k in range(tile)]
            base = e0 - t0 - tile + 1
            rhs = [
                second[base + k] if base + k >= 0 else None for k in range(2 * tile - 1)
            ]
            for de in range(tile):
                for dt in range(tile):
                    other = rhs[de - dt + tile - 1]
                    if other is None:
                        continue
                    term = lhs[dt] * other
                    totals[de] = term if totals[de] is None else totals[de] + term
        for de in range(0, tile, 2):
            pair = jnp.concatenate([totals[de], totals[de + 1]], axis=0) * scale
            out[pl.ds((e0 + de) * ROWS, 2 * ROWS), :] = pair.astype(jnp.bfloat16)


def screen_kernel(blocks, orbitals, packed, out):
    order = out.shape[1]
    half = order // 2
    rest = packed[2 * order : 2 * order + half, :]
    width = order - LANES
    for b in range(2):
        left = orbitals[blocks[b, 0]]
        right = orbitals[blocks[b, 1]]
        at = 2 * b * width
        tail = jnp.concatenate(
            [rest[:, at : at + width], rest[:, at + width : at + 2 * width]], axis=0
        )
        polar = jnp.concatenate([packed[b * order : (b + 1) * order, :], tail], axis=1)
        screened = matmul(left, polar).astype(jnp.bfloat16)
        out[b] = matmul_t(screened, right).astype(jnp.bfloat16)


def onchip(value):
    return pltpu.with_memory_space_constraint(value, pltpu.VMEM)


def per_device(orbitals, couplings, blocks, partner):
    axes = ("wide", "sub")
    energies = lax.axis_size("wide") * lax.axis_size("sub")
    pairs = lax.axis_size("pair")
    order = couplings.shape[1]
    packed_rows = 2 * order * order // LANES
    shifted = lax.ppermute(
        couplings, "pair", [(i, (i + pairs // 2) % pairs) for i in range(pairs)]
    )
    sites = onchip(orbitals.reshape(orbitals.shape[0], order, order))
    here = onchip(couplings)
    direct = pl.pallas_call(
        direct_kernel,
        out_shape=pltpu.VMEM((packed_rows, LANES), jnp.bfloat16),
        in_specs=[SMEM, VMEM, VMEM],
        out_specs=VMEM,
        name="direct",
    )(blocks, sites, here)
    outgoing = pl.pallas_call(
        mirror_kernel,
        out_shape=pltpu.VMEM((energies, 2 * ROWS, LANES), jnp.bfloat16),
        in_specs=[SMEM, SMEM, VMEM, VMEM, VMEM],
        out_specs=VMEM,
        name="mirror",
    )(blocks, partner, sites, onchip(shifted), onchip(direct))
    incoming = lax.all_to_all(outgoing, axes, split_axis=0, concat_axis=0, tiled=True)
    polar = pl.pallas_call(
        functools.partial(convolve_kernel, 8),
        out_shape=pltpu.VMEM((energies * ROWS, LANES), jnp.bfloat16),
        in_specs=[VMEM],
        out_specs=VMEM,
        scratch_shapes=[pltpu.VMEM((energies, ROWS, LANES), jnp.float32)] * 2,
        name="convolve",
    )(onchip(incoming))
    returned = lax.all_to_all(
        polar.reshape(energies, ROWS, LANES), axes, split_axis=0, concat_axis=0, tiled=True
    )
    result = pl.pallas_call(
        screen_kernel,
        out_shape=jax.ShapeDtypeStruct(couplings.shape, jnp.bfloat16),
        in_specs=[SMEM, VMEM, VMEM],
        out_specs=VMEM,
        name="screen",
    )(blocks, sites, onchip(returned.reshape(energies * ROWS, LANES)))
    return result.reshape(couplings.shape[0], 1, order, order)


def solution(mesh):
    placed = (
        P(None, ("wide", "sub"), None, None),
        P("pair", None, None),
        P("pair", None),
        P("pair"),
    )
    return jax.shard_map(
        per_device,
        mesh=mesh,
        in_specs=placed,
        out_specs=P("pair", ("wide", "sub"), None, None),
        check_vma=False,
    )
```

```python
import functools

import jax
import jax.numpy as jnp
from jax import lax
from jax.experimental import pallas as pl
from jax.experimental.pallas import tpu as pltpu
from jax.sharding import Mesh
from jax.sharding import PartitionSpec as P

LANES = 128
ROWS = 8
VMEM = pl.BlockSpec(memory_space=pltpu.VMEM)
SMEM = pl.BlockSpec(memory_space=pltpu.SMEM)


def matmul(left, right):
    return jnp.dot(left, right, preferred_element_type=jnp.float32)


def matmul_t(left, right):
    return lax.dot_general(
        left, right, (((1,), (1,)), ((), ())), preferred_element_type=jnp.float32
    )


def pack(first, second):
    half = first.shape[0] // 2
    rest = jnp.concatenate(
        [
            first[:half, LANES:],
            first[half:, LANES:],
            second[:half, LANES:],
            second[half:, LANES:],
        ],
        axis=1,
    )
    return jnp.concatenate([first[:, :LANES], second[:, :LANES], rest], axis=0)


def direct_kernel(total, blocks, partner, orbitals, couplings, out, inner):
    groups = out.shape[0] // 2
    used = 2 * couplings.shape[1] * couplings.shape[2] // (ROWS * LANES)
    low = lax.select(partner[0] < total // 2, 1, 0)
    results = []
    for b in range(2):
        left = orbitals[blocks[b, 0]]
        right = orbitals[blocks[b, 1]]
        inner[b] = matmul(left, couplings[b]).astype(jnp.bfloat16)
        results.append(matmul_t(inner[b], right))
    flat = pack(*results).astype(jnp.bfloat16)
    out[pl.ds(low * groups, used)] = flat.reshape(used, ROWS, LANES)
    first = lax.rem(partner[0], 2)
    results = []
    for b in (first, 1 - first):
        results.append(matmul_t(orbitals[blocks[b, 1]], inner[b]))
    flat = pack(*results).astype(jnp.bfloat16)
    out[pl.ds((1 - low) * groups, used)] = flat.reshape(used, ROWS, LANES)
    rest = jnp.zeros((groups - used, ROWS, LANES), jnp.bfloat16)
    out[used:groups] = rest
    out[groups + used :] = rest


def convolve_kernel(tile, incoming, out, first, second):
    count = incoming.shape[0] // 2
    first[...] = incoming[:count].astype(jnp.float32)
    second[...] = incoming[count:].astype(jnp.float32)
    scale = count ** (-0.5)
    for e0 in range(0, count, tile):
        totals = [None] * tile
        for t0 in range(0, e0 + tile, tile):
            lhs = [first[t0 + k] for k in range(tile)]
            base = e0 - t0 - tile + 1
            rhs = [
                second[base + k] if base + k >= 0 else None for k in range(2 * tile - 1)
            ]
            for de in range(tile):
                for dt in range(tile):
                    other = rhs[de - dt + tile - 1]
                    if other is None:
                        continue
                    term = lhs[dt] * other
                    totals[de] = term if totals[de] is None else totals[de] + term
        for de in range(0, tile, 2):
            pair = jnp.concatenate([totals[de], totals[de + 1]], axis=0) * scale
            out[pl.ds((e0 + de) * ROWS, 2 * ROWS), :] = pair.astype(jnp.bfloat16)


def screen_kernel(blocks, orbitals, packed, out):
    order = out.shape[1]
    half = order // 2
    rest = packed[2 * order : 2 * order + half, :]
    width = order - LANES
    for b in range(2):
        left = orbitals[blocks[b, 0]]
        right = orbitals[blocks[b, 1]]
        at = 2 * b * width
        tail = jnp.concatenate(
            [rest[:, at : at + width], rest[:, at + width : at + 2 * width]], axis=0
        )
        polar = jnp.concatenate([packed[b * order : (b + 1) * order, :], tail], axis=1)
        screened = matmul(left, polar).astype(jnp.bfloat16)
        out[b] = matmul_t(screened, right).astype(jnp.bfloat16)


def onchip(value):
    return pltpu.with_memory_space_constraint(value, pltpu.VMEM)


def per_device(total, orbitals, couplings, blocks, partner):
    axes = ("wide", "sub")
    energies = lax.axis_size("wide") * lax.axis_size("sub")
    order = couplings.shape[1]
    sites = onchip(orbitals.reshape(orbitals.shape[0], order, order))
    outgoing = pl.pallas_call(
        functools.partial(direct_kernel, total),
        out_shape=pltpu.VMEM((2 * energies, ROWS, LANES), jnp.bfloat16),
        in_specs=[SMEM, SMEM, VMEM, VMEM],
        out_specs=VMEM,
        scratch_shapes=[pltpu.VMEM(couplings.shape, jnp.bfloat16)],
        name="direct",
    )(blocks, partner, sites, onchip(couplings))
    incoming = lax.all_to_all(
        outgoing, ("half",) + axes, split_axis=0, concat_axis=0, tiled=True
    )
    polar = pl.pallas_call(
        functools.partial(convolve_kernel, 8),
        out_shape=pltpu.VMEM((energies * ROWS, LANES), jnp.bfloat16),
        in_specs=[VMEM],
        out_specs=VMEM,
        scratch_shapes=[pltpu.VMEM((energies, ROWS, LANES), jnp.float32)] * 2,
        name="convolve",
    )(onchip(incoming))
    returned = lax.all_to_all(
        polar.reshape(energies, ROWS, LANES), axes, split_axis=0, concat_axis=0, tiled=True
    )
    result = pl.pallas_call(
        screen_kernel,
        out_shape=jax.ShapeDtypeStruct(couplings.shape, jnp.bfloat16),
        in_specs=[SMEM, VMEM, VMEM],
        out_specs=VMEM,
        name="screen",
    )(blocks, sites, onchip(returned.reshape(energies * ROWS, LANES)))
    return result.reshape(couplings.shape[0], 1, order, order)


def solution(mesh):
    sizes = mesh.shape
    pairs = sizes["pair"]
    halved = Mesh(
        mesh.devices.reshape(sizes["wide"], 2, pairs // 2, sizes["sub"]),
        ("wide", "half", "inside", "sub"),
    )
    pair = ("half", "inside")
    placed = (
        P(None, ("wide", "sub"), None, None),
        P(pair, None, None),
        P(pair, None),
        P(pair),
    )
    return jax.shard_map(
        functools.partial(per_device, 2 * pairs),
        mesh=halved,
        in_specs=placed,
        out_specs=P(pair, ("wide", "sub"), None, None),
        check_vma=False,
    )
```

```python
import functools

import jax
import jax.numpy as jnp
from jax import lax
from jax.experimental import pallas as pl
from jax.experimental.pallas import tpu as pltpu
from jax.sharding import PartitionSpec as P


LANES = 128
ROWS = 8
VMEM = pl.BlockSpec(memory_space=pltpu.VMEM)
SMEM = pl.BlockSpec(memory_space=pltpu.SMEM)


def matmul(left, right):
    return jnp.dot(left, right, preferred_element_type=jnp.float32)


def matmul_t(left, right):
    return lax.dot_general(
        left, right, (((1,), (1,)), ((), ())), preferred_element_type=jnp.float32
    )


def pack(first, second):
    half = first.shape[0] // 2
    rest = jnp.concatenate(
        [
            first[:half, LANES:],
            first[half:, LANES:],
            second[:half, LANES:],
            second[half:, LANES:],
        ],
        axis=1,
    )
    return jnp.concatenate([first[:, :LANES], second[:, :LANES], rest], axis=0)


def put(out, matrices):
    flat = pack(*matrices).astype(jnp.bfloat16)
    used = flat.shape[0] // ROWS
    out[:used] = flat.reshape(used, ROWS, LANES)
    out[used:] = jnp.zeros((out.shape[0] - used, ROWS, LANES), jnp.bfloat16)


def direct_kernel(blocks, orbitals, couplings, out):
    results = []
    for b in range(2):
        left = orbitals[blocks[b, 0]]
        right = orbitals[blocks[b, 1]]
        inner = matmul(left, couplings[b]).astype(jnp.bfloat16)
        results.append(matmul_t(inner, right))
    put(out, results)


def mirror_kernel(blocks, partner, orbitals, shifted, out):
    results = []
    for b in range(2):
        left = orbitals[blocks[b, 0]]
        right = orbitals[blocks[b, 1]]
        across = matmul(right, shifted[lax.rem(partner[b], 2)]).astype(jnp.bfloat16)
        results.append(matmul_t(left, across))
    put(out, results)


def widen_kernel(value, out):
    out[...] = value[...].astype(jnp.float32)


def convolve_kernel(tile, first, mirror, out, second):
    count = first.shape[0]
    second[...] = mirror[...].astype(jnp.float32)
    scale = count ** (-0.5)
    for e0 in range(0, count, tile):
        totals = [None] * tile
        for t0 in range(0, e0 + tile, tile):
            lhs = [first[t0 + k] for k in range(tile)]
            base = e0 - t0 - tile + 1
            rhs = [
                second[base + k] if base + k >= 0 else None for k in range(2 * tile - 1)
            ]
            for de in range(tile):
                for dt in range(tile):
                    other = rhs[de - dt + tile - 1]
                    if other is None:
                        continue
                    term = lhs[dt] * other
                    totals[de] = term if totals[de] is None else totals[de] + term
        for de in range(0, tile, 2):
            pair = jnp.concatenate([totals[de], totals[de + 1]], axis=0) * scale
            out[pl.ds((e0 + de) * ROWS, 2 * ROWS), :] = pair.astype(jnp.bfloat16)


def screen_kernel(blocks, orbitals, packed, out):
    order = out.shape[1]
    half = order // 2
    rest = packed[2 * order : 2 * order + half, :]
    width = order - LANES
    for b in range(2):
        left = orbitals[blocks[b, 0]]
        right = orbitals[blocks[b, 1]]
        at = 2 * b * width
        tail = jnp.concatenate(
            [rest[:, at : at + width], rest[:, at + width : at + 2 * width]], axis=0
        )
        polar = jnp.concatenate([packed[b * order : (b + 1) * order, :], tail], axis=1)
        screened = matmul(left, polar).astype(jnp.bfloat16)
        out[b] = matmul_t(screened, right).astype(jnp.bfloat16)


def onchip(value):
    return pltpu.with_memory_space_constraint(value, pltpu.VMEM)


def per_device(orbitals, couplings, blocks, partner):
    axes = ("wide", "sub")
    energies = lax.axis_size("wide") * lax.axis_size("sub")
    pairs = lax.axis_size("pair")
    order = couplings.shape[1]

    def exchange(value):
        return lax.all_to_all(value, axes, split_axis=0, concat_axis=0, tiled=True)

    slots = pltpu.VMEM((energies, ROWS, LANES), jnp.bfloat16)
    shifted = lax.ppermute(
        couplings, "pair", [(i, (i + pairs // 2) % pairs) for i in range(pairs)]
    )
    sites = onchip(orbitals.reshape(orbitals.shape[0], order, order))
    direct = pl.pallas_call(
        direct_kernel,
        out_shape=slots,
        in_specs=[SMEM, VMEM, VMEM],
        out_specs=VMEM,
        name="direct",
    )(blocks, sites, onchip(couplings))
    direct = exchange(direct)
    direct = pl.pallas_call(
        widen_kernel,
        out_shape=pltpu.VMEM((energies, ROWS, LANES), jnp.float32),
        in_specs=[VMEM],
        out_specs=VMEM,
        name="widen",
    )(onchip(direct))
    mirror = pl.pallas_call(
        mirror_kernel,
        out_shape=slots,
        in_specs=[SMEM, SMEM, VMEM, VMEM],
        out_specs=VMEM,
        name="mirror",
    )(blocks, partner, sites, onchip(shifted))
    mirror = exchange(mirror)
    polar = pl.pallas_call(
        functools.partial(convolve_kernel, 8),
        out_shape=pltpu.VMEM((energies * ROWS, LANES), jnp.bfloat16),
        in_specs=[VMEM, VMEM],
        out_specs=VMEM,
        scratch_shapes=[pltpu.VMEM((energies, ROWS, LANES), jnp.float32)],
        name="convolve",
    )(onchip(direct), onchip(mirror))
    returned = exchange(polar.reshape(energies, ROWS, LANES))
    result = pl.pallas_call(
        screen_kernel,
        out_shape=jax.ShapeDtypeStruct(couplings.shape, jnp.bfloat16),
        in_specs=[SMEM, VMEM, VMEM],
        out_specs=VMEM,
        name="screen",
    )(blocks, sites, onchip(returned.reshape(energies * ROWS, LANES)))
    return result.reshape(couplings.shape[0], 1, order, order)


def solution(mesh):
    placed = (
        P(None, ("wide", "sub"), None, None),
        P("pair", None, None),
        P("pair", None),
        P("pair"),
    )
    return jax.shard_map(
        per_device,
        mesh=mesh,
        in_specs=placed,
        out_specs=P("pair", ("wide", "sub"), None, None),
        check_vma=False,
    )
```

```python
import functools

import jax
import jax.numpy as jnp
from jax import lax
from jax.experimental import pallas as pl
from jax.experimental.pallas import tpu as pltpu
from jax.sharding import PartitionSpec as P

LANES = 128
ROWS = 8
VMEM = pl.BlockSpec(memory_space=pltpu.VMEM)
SMEM = pl.BlockSpec(memory_space=pltpu.SMEM)


def matmul(left, right):
    return jnp.dot(left, right, preferred_element_type=jnp.float32)


def matmul_t(left, right):
    return lax.dot_general(
        left, right, (((1,), (1,)), ((), ())), preferred_element_type=jnp.float32
    )


def pack(first, second):
    half = first.shape[0] // 2
    rest = jnp.concatenate(
        [
            first[:half, LANES:],
            first[half:, LANES:],
            second[:half, LANES:],
            second[half:, LANES:],
        ],
        axis=1,
    )
    return jnp.concatenate([first[:, :LANES], second[:, :LANES], rest], axis=0)


def unpack(packed, order, b):
    half = order // 2
    width = order - LANES
    rest = packed[2 * order : 2 * order + half, :]
    at = 2 * b * width
    tail = jnp.concatenate(
        [rest[:, at : at + width], rest[:, at + width : at + 2 * width]], axis=0
    )
    return jnp.concatenate([packed[b * order : (b + 1) * order, :], tail], axis=1)


def send_kernel(partner, couplings, out):
    first = lax.rem(partner[0], 2)
    out[...] = pack(couplings[first], couplings[1 - first])


def direct_kernel(blocks, orbitals, couplings, out, factors):
    results = []
    for b in range(2):
        left = orbitals[blocks[b, 0]]
        right = orbitals[blocks[b, 1]]
        factors[2 * b] = left
        factors[2 * b + 1] = right
        inner = matmul(left, couplings[b]).astype(jnp.bfloat16)
        results.append(matmul_t(inner, right))
    out[...] = pack(*results).astype(jnp.bfloat16)


def mirror_kernel(factors, shifted, direct, out):
    results = []
    for b in range(2):
        coupling = unpack(shifted, factors.shape[1], b)
        across = matmul(factors[2 * b + 1], coupling).astype(jnp.bfloat16)
        results.append(matmul_t(factors[2 * b], across))
    mirror = pack(*results)
    used = direct.shape[0] // ROWS
    both = jnp.concatenate(
        [
            direct[...].astype(jnp.float32).reshape(used, ROWS, LANES),
            mirror.reshape(used, ROWS, LANES),
        ],
        axis=1,
    )
    out[:used] = both.astype(jnp.bfloat16)
    out[used:] = jnp.zeros((out.shape[0] - used, 2 * ROWS, LANES), jnp.bfloat16)


def convolve_kernel(tile, incoming, out, first, second):
    count = incoming.shape[0]
    both = incoming[...].astype(jnp.float32)
    first[...] = both[:, :ROWS]
    second[...] = both[:, ROWS:]
    scale = count ** (-0.5)
    for e0 in range(0, count, tile):
        totals = [None] * tile
        for t0 in range(0, e0 + tile, tile):
            lhs = [first[t0 + k] for k in range(tile)]
            base = e0 - t0 - tile + 1
            rhs = [
                second[base + k] if base + k >= 0 else None for k in range(2 * tile - 1)
            ]
            for de in range(tile):
                for dt in range(tile):
                    other = rhs[de - dt + tile - 1]
                    if other is None:
                        continue
                    term = lhs[dt] * other
                    totals[de] = term if totals[de] is None else totals[de] + term
        for de in range(0, tile, 2):
            pair = jnp.concatenate([totals[de], totals[de + 1]], axis=0) * scale
            out[pl.ds((e0 + de) * ROWS, 2 * ROWS), :] = pair.astype(jnp.bfloat16)


def screen_kernel(factors, packed, out, held, sems):
    copies = []
    for b in range(2):
        polar = unpack(packed, held.shape[1], b)
        screened = matmul(factors[2 * b], polar).astype(jnp.bfloat16)
        held[b] = matmul_t(screened, factors[2 * b + 1]).astype(jnp.bfloat16)
        copy = pltpu.make_async_copy(held.at[b], out.at[b], sems.at[b])
        copy.start()
        copies.append(copy)
    for copy in copies:
        copy.wait()


def onchip(value):
    return pltpu.with_memory_space_constraint(value, pltpu.VMEM)


def per_device(orbitals, couplings, blocks, partner):
    axes = ("wide", "sub")
    energies = lax.axis_size("wide") * lax.axis_size("sub")
    pairs = lax.axis_size("pair")
    order = couplings.shape[1]
    packed_rows = 2 * order * order // LANES
    packed = pltpu.VMEM((packed_rows, LANES), jnp.bfloat16)
    leaving = pl.pallas_call(
        send_kernel,
        out_shape=packed,
        in_specs=[SMEM, VMEM],
        out_specs=VMEM,
        name="send",
    )(partner, couplings)
    shifted = lax.ppermute(
        leaving, "pair", [(i, (i + pairs // 2) % pairs) for i in range(pairs)]
    )
    sites = orbitals.reshape(orbitals.shape[0], order, order)
    direct, factors = pl.pallas_call(
        direct_kernel,
        out_shape=[packed, pltpu.VMEM((4, order, order), jnp.bfloat16)],
        in_specs=[SMEM, VMEM, VMEM],
        out_specs=[VMEM, VMEM],
        name="direct",
    )(blocks, onchip(sites), onchip(couplings))
    outgoing = pl.pallas_call(
        mirror_kernel,
        out_shape=pltpu.VMEM((energies, 2 * ROWS, LANES), jnp.bfloat16),
        in_specs=[VMEM, VMEM, VMEM],
        out_specs=VMEM,
        name="mirror",
    )(onchip(factors), onchip(shifted), onchip(direct))
    incoming = lax.all_to_all(outgoing, axes, split_axis=0, concat_axis=0, tiled=True)
    polar = pl.pallas_call(
        functools.partial(convolve_kernel, 8),
        out_shape=pltpu.VMEM((energies * ROWS, LANES), jnp.bfloat16),
        in_specs=[VMEM],
        out_specs=VMEM,
        scratch_shapes=[pltpu.VMEM((energies, ROWS, LANES), jnp.float32)] * 2,
        name="convolve",
    )(onchip(incoming))
    returned = lax.all_to_all(
        polar.reshape(energies, ROWS, LANES), axes, split_axis=0, concat_axis=0, tiled=True
    )
    result = pl.pallas_call(
        screen_kernel,
        out_shape=jax.ShapeDtypeStruct(couplings.shape, jnp.bfloat16),
        in_specs=[VMEM, VMEM],
        out_specs=pl.BlockSpec(memory_space=pl.ANY),
        scratch_shapes=[
            pltpu.VMEM(couplings.shape, jnp.bfloat16),
            pltpu.SemaphoreType.DMA((2,)),
        ],
        name="screen",
    )(onchip(factors), onchip(returned.reshape(energies * ROWS, LANES)))
    return result.reshape(couplings.shape[0], 1, order, order)


def solution(mesh):
    placed = (
        P(None, ("wide", "sub"), None, None),
        P("pair", None, None),
        P("pair", None),
        P("pair"),
    )
    return jax.shard_map(
        per_device,
        mesh=mesh,
        in_specs=placed,
        out_specs=P("pair", ("wide", "sub"), None, None),
        check_vma=False,
    )
```

```python
import functools

import jax
import jax.numpy as jnp
from jax import lax
from jax.experimental import pallas as pl
from jax.experimental.pallas import tpu as pltpu
from jax.sharding import PartitionSpec as P

LANES = 128
ROWS = 8
VMEM = pl.BlockSpec(memory_space=pltpu.VMEM)
SMEM = pl.BlockSpec(memory_space=pltpu.SMEM)


def matmul(left, right):
    return jnp.dot(left, right, preferred_element_type=jnp.float32)


def matmul_t(left, right):
    return lax.dot_general(
        left, right, (((1,), (1,)), ((), ())), preferred_element_type=jnp.float32
    )


def pack(first, second):
    half = first.shape[0] // 2
    rest = jnp.concatenate(
        [
            first[:half, LANES:],
            first[half:, LANES:],
            second[:half, LANES:],
            second[half:, LANES:],
        ],
        axis=1,
    )
    return jnp.concatenate([first[:, :LANES], second[:, :LANES], rest], axis=0)


def unpack(packed, order, b):
    half = order // 2
    width = order - LANES
    rest = packed[2 * order : 2 * order + half, :]
    at = 2 * b * width
    tail = jnp.concatenate(
        [rest[:, at : at + width], rest[:, at + width : at + 2 * width]], axis=0
    )
    return jnp.concatenate([packed[b * order : (b + 1) * order, :], tail], axis=1)


def send_kernel(couplings, out):
    out[...] = pack(couplings[0], couplings[1])


def direct_kernel(blocks, partner, orbitals, couplings, out, factors, arriving, crossed):
    first = lax.rem(partner[0], 2)
    results = []
    for b in range(2):
        left = orbitals[blocks[b, 0]]
        right = orbitals[blocks[b, 1]]
        slot = first if b == 0 else 1 - first
        for side, factor in enumerate((left, right)):
            factors[2 * b + side] = factor
            arriving[2 * slot + side] = factor
        inner = matmul(left, couplings[b]).astype(jnp.bfloat16)
        results.append(matmul_t(inner, right))
    out[...] = pack(*results).astype(jnp.bfloat16)
    crossed[...] = jnp.full(crossed.shape, first, jnp.int32)


def mirror_kernel(factors, crossed, shifted, direct, out):
    results = []
    for b in range(2):
        coupling = unpack(shifted, factors.shape[1], b)
        across = matmul(factors[2 * b + 1], coupling).astype(jnp.bfloat16)
        results.append(matmul_t(factors[2 * b], across))
    arrived = pack(*results)
    order = factors.shape[1]
    swap = jnp.broadcast_to(crossed[0:1, :], arrived.shape) > 0
    half = (order - LANES) * 2
    rest = arrived[2 * order :]
    turned = jnp.concatenate(
        [
            arrived[order : 2 * order],
            arrived[:order],
            jnp.concatenate([rest[:, half:], rest[:, :half]], axis=1),
        ],
        axis=0,
    )
    mirror = jnp.where(swap, turned, arrived)
    used = direct.shape[0] // ROWS
    both = jnp.concatenate(
        [
            direct[...].astype(jnp.float32).reshape(used, ROWS, LANES),
            mirror.reshape(used, ROWS, LANES),
        ],
        axis=1,
    )
    out[:used] = both.astype(jnp.bfloat16)
    out[used:] = jnp.zeros((out.shape[0] - used, 2 * ROWS, LANES), jnp.bfloat16)


def convolve_kernel(tile, incoming, out, first, second):
    count = incoming.shape[0]
    both = incoming[...].astype(jnp.float32)
    first[...] = both[:, :ROWS]
    second[...] = both[:, ROWS:]
    scale = count ** (-0.5)
    for e0 in range(0, count, tile):
        totals = [None] * tile
        for t0 in range(0, e0 + tile, tile):
            lhs = [first[t0 + k] for k in range(tile)]
            base = e0 - t0 - tile + 1
            rhs = [
                second[base + k] if base + k >= 0 else None for k in range(2 * tile - 1)
            ]
            for de in range(tile):
                for dt in range(tile):
                    other = rhs[de - dt + tile - 1]
                    if other is None:
                        continue
                    term = lhs[dt] * other
                    totals[de] = term if totals[de] is None else totals[de] + term
        for de in range(0, tile, 2):
            pair = jnp.concatenate([totals[de], totals[de + 1]], axis=0) * scale
            out[pl.ds((e0 + de) * ROWS, 2 * ROWS), :] = pair.astype(jnp.bfloat16)


def screen_kernel(factors, packed, out, held, sems):
    copies = []
    for b in range(2):
        polar = unpack(packed, held.shape[1], b)
        screened = matmul(factors[2 * b], polar).astype(jnp.bfloat16)
        held[b] = matmul_t(screened, factors[2 * b + 1]).astype(jnp.bfloat16)
        copy = pltpu.make_async_copy(held.at[b], out.at[b], sems.at[b])
        copy.start()
        copies.append(copy)
    for copy in copies:
        copy.wait()


def onchip(value):
    return pltpu.with_memory_space_constraint(value, pltpu.VMEM)


def per_device(orbitals, couplings, blocks, partner):
    axes = ("wide", "sub")
    energies = lax.axis_size("wide") * lax.axis_size("sub")
    pairs = lax.axis_size("pair")
    order = couplings.shape[1]
    packed_rows = 2 * order * order // LANES
    packed = pltpu.VMEM((packed_rows, LANES), jnp.bfloat16)
    leaving = pl.pallas_call(
        send_kernel,
        out_shape=packed,
        in_specs=[VMEM],
        out_specs=VMEM,
        name="send",
    )(couplings)
    shifted = lax.ppermute(
        leaving, "pair", [(i, (i + pairs // 2) % pairs) for i in range(pairs)]
    )
    sites = orbitals.reshape(orbitals.shape[0], order, order)
    chosen = pltpu.VMEM((4, order, order), jnp.bfloat16)
    direct, factors, arriving, crossed = pl.pallas_call(
        direct_kernel,
        out_shape=[packed, chosen, chosen, pltpu.VMEM((ROWS, LANES), jnp.int32)],
        in_specs=[SMEM, SMEM, VMEM, VMEM],
        out_specs=[VMEM] * 4,
        name="direct",
    )(blocks, partner, onchip(sites), onchip(couplings))
    outgoing = pl.pallas_call(
        mirror_kernel,
        out_shape=pltpu.VMEM((energies, 2 * ROWS, LANES), jnp.bfloat16),
        in_specs=[VMEM] * 4,
        out_specs=VMEM,
        name="mirror",
    )(onchip(arriving), onchip(crossed), onchip(shifted), onchip(direct))
    incoming = lax.all_to_all(outgoing, axes, split_axis=0, concat_axis=0, tiled=True)
    polar = pl.pallas_call(
        functools.partial(convolve_kernel, 8),
        out_shape=pltpu.VMEM((energies * ROWS, LANES), jnp.bfloat16),
        in_specs=[VMEM],
        out_specs=VMEM,
        scratch_shapes=[pltpu.VMEM((energies, ROWS, LANES), jnp.float32)] * 2,
        name="convolve",
    )(onchip(incoming))
    returned = lax.all_to_all(
        polar.reshape(energies, ROWS, LANES), axes, split_axis=0, concat_axis=0, tiled=True
    )
    result = pl.pallas_call(
        screen_kernel,
        out_shape=jax.ShapeDtypeStruct(couplings.shape, jnp.bfloat16),
        in_specs=[VMEM, VMEM],
        out_specs=pl.BlockSpec(memory_space=pl.ANY),
        scratch_shapes=[
            pltpu.VMEM(couplings.shape, jnp.bfloat16),
            pltpu.SemaphoreType.DMA((2,)),
        ],
        name="screen",
    )(onchip(factors), onchip(returned.reshape(energies * ROWS, LANES)))
    return result.reshape(couplings.shape[0], 1, order, order)


def solution(mesh):
    placed = (
        P(None, ("wide", "sub"), None, None),
        P("pair", None, None),
        P("pair", None),
        P("pair"),
    )
    return jax.shard_map(
        per_device,
        mesh=mesh,
        in_specs=placed,
        out_specs=P("pair", ("wide", "sub"), None, None),
        check_vma=False,
    )
```

```python
import functools

import jax
import jax.numpy as jnp
from jax import lax
from jax.experimental import pallas as pl
from jax.experimental.pallas import tpu as pltpu
from jax.sharding import PartitionSpec as P


LANES = 128
ROWS = 8
VMEM = pl.BlockSpec(memory_space=pltpu.VMEM)
SMEM = pl.BlockSpec(memory_space=pltpu.SMEM)


def matmul(left, right):
    return jnp.dot(left, right, preferred_element_type=jnp.float32)


def matmul_t(left, right):
    return lax.dot_general(
        left, right, (((1,), (1,)), ((), ())), preferred_element_type=jnp.float32
    )


def pack(first, second):
    half = first.shape[0] // 2
    rest = jnp.concatenate(
        [
            first[:half, LANES:],
            first[half:, LANES:],
            second[:half, LANES:],
            second[half:, LANES:],
        ],
        axis=1,
    )
    return jnp.concatenate([first[:, :LANES], second[:, :LANES], rest], axis=0)


def unpack(packed, order, b):
    half = order // 2
    width = order - LANES
    rest = packed[2 * order : 2 * order + half, :]
    at = 2 * b * width
    tail = jnp.concatenate(
        [rest[:, at : at + width], rest[:, at + width : at + 2 * width]], axis=0
    )
    return jnp.concatenate([packed[b * order : (b + 1) * order, :], tail], axis=1)


def send_kernel(couplings, out):
    out[...] = pack(couplings[0], couplings[1])


def direct_kernel(blocks, partner, orbitals, couplings, out, factors, arriving, crossed):
    first = lax.rem(partner[0], 2)
    results = []
    for b in range(2):
        left = orbitals[blocks[b, 0]]
        right = orbitals[blocks[b, 1]]
        slot = first if b == 0 else 1 - first
        for side, factor in enumerate((left, right)):
            factors[2 * b + side] = factor
            arriving[2 * slot + side] = factor
        inner = matmul(left, couplings[b]).astype(jnp.bfloat16)
        results.append(matmul_t(inner, right))
    out[...] = pack(*results).astype(jnp.bfloat16)
    crossed[...] = jnp.full(crossed.shape, first, jnp.int32)


def mirror_kernel(factors, crossed, shifted, direct, out):
    results = []
    for b in range(2):
        coupling = unpack(shifted, factors.shape[1], b)
        across = matmul(factors[2 * b + 1], coupling).astype(jnp.bfloat16)
        results.append(matmul_t(factors[2 * b], across))
    arrived = pack(*results)
    order = factors.shape[1]
    swap = jnp.broadcast_to(crossed[0:1, :], arrived.shape) > 0
    half = (order - LANES) * 2
    rest = arrived[2 * order :]
    turned = jnp.concatenate(
        [
            arrived[order : 2 * order],
            arrived[:order],
            jnp.concatenate([rest[:, half:], rest[:, :half]], axis=1),
        ],
        axis=0,
    )
    mirror = jnp.where(swap, turned, arrived)
    used = direct.shape[0] // ROWS
    both = jnp.concatenate(
        [
            direct[...].astype(jnp.float32).reshape(used, ROWS, LANES),
            mirror.reshape(used, ROWS, LANES),
        ],
        axis=1,
    )
    out[:used] = both.astype(jnp.bfloat16)
    out[used:] = jnp.zeros((out.shape[0] - used, 2 * ROWS, LANES), jnp.bfloat16)


def convolve_kernel(tile, incoming, out, first, second):
    count = incoming.shape[0]
    both = incoming[...].astype(jnp.float32)
    first[...] = both[:, :ROWS]
    second[...] = both[:, ROWS:]
    scale = count ** (-0.5)
    for e0 in range(0, count, tile):
        totals = [None] * tile
        for t0 in range(0, e0 + tile, tile):
            lhs = [first[t0 + k] for k in range(tile)]
            base = e0 - t0 - tile + 1
            rhs = [
                second[base + k] if base + k >= 0 else None for k in range(2 * tile - 1)
            ]
            for de in range(tile):
                for dt in range(tile):
                    other = rhs[de - dt + tile - 1]
                    if other is None:
                        continue
                    term = lhs[dt] * other
                    totals[de] = term if totals[de] is None else totals[de] + term
        for de in range(0, tile, 2):
            pair = jnp.concatenate([totals[de], totals[de + 1]], axis=0) * scale
            out[pl.ds((e0 + de) * ROWS, 2 * ROWS), :] = pair.astype(jnp.bfloat16)


def screen_kernel(factors, packed, out, held, sems):
    copies = []
    for b in range(2):
        polar = unpack(packed, held.shape[1], b)
        screened = matmul(factors[2 * b], polar).astype(jnp.bfloat16)
        held[b] = matmul_t(screened, factors[2 * b + 1]).astype(jnp.bfloat16)
        copy = pltpu.make_async_copy(held.at[b], out.at[b], sems.at[b])
        copy.start()
        copies.append(copy)
    for copy in copies:
        copy.wait()


def onchip(value):
    return pltpu.with_memory_space_constraint(value, pltpu.VMEM)


def per_device(orbitals, couplings, blocks, partner):
    axes = ("wide", "sub")
    energies = lax.axis_size("wide") * lax.axis_size("sub")
    pairs = lax.axis_size("pair")
    order = couplings.shape[1]
    packed_rows = 2 * order * order // LANES
    packed = pltpu.VMEM((packed_rows, LANES), jnp.bfloat16)
    leaving = pl.pallas_call(
        send_kernel,
        out_shape=packed,
        in_specs=[VMEM],
        out_specs=VMEM,
        name="send",
    )(couplings)
    near = pairs // 2
    early = lax.axis_index("pair") < near
    from_late = lax.ppermute(leaving, "pair", [(i + near, i) for i in range(near)])
    from_early = lax.ppermute(leaving, "pair", [(i, i + near) for i in range(near)])
    sites = orbitals.reshape(orbitals.shape[0], order, order)
    chosen = pltpu.VMEM((4, order, order), jnp.bfloat16)
    direct, factors, arriving, crossed = pl.pallas_call(
        direct_kernel,
        out_shape=[packed, chosen, chosen, pltpu.VMEM((ROWS, LANES), jnp.int32)],
        in_specs=[SMEM, SMEM, VMEM, VMEM],
        out_specs=[VMEM] * 4,
        name="direct",
    )(blocks, partner, sites, couplings)
    result = pltpu.VMEM((energies * ROWS, LANES), jnp.bfloat16)

    def polarize(polar, shifted, direct, arriving, crossed):
        outgoing = pl.pallas_call(
            mirror_kernel,
            out_shape=pltpu.VMEM((energies, 2 * ROWS, LANES), jnp.bfloat16),
            in_specs=[VMEM] * 4,
            out_specs=VMEM,
            name="mirror",
        )(onchip(arriving), onchip(crossed), onchip(shifted), onchip(direct))
        incoming = lax.all_to_all(outgoing, axes, split_axis=0, concat_axis=0, tiled=True)
        return pl.pallas_call(
            functools.partial(convolve_kernel, 8),
            out_shape=result,
            in_specs=[VMEM],
            out_specs=VMEM,
            scratch_shapes=[pltpu.VMEM((energies, ROWS, LANES), jnp.float32)] * 2,
            name="convolve",
        )(onchip(incoming))

    def keep(polar, *_):
        return polar

    polar = jnp.zeros((energies * ROWS, LANES), jnp.bfloat16)
    polar = lax.cond(early, polarize, keep, polar, from_late, direct, arriving, crossed)
    polar = lax.cond(early, keep, polarize, polar, from_early, direct, arriving, crossed)
    returned = lax.all_to_all(
        polar.reshape(energies, ROWS, LANES), axes, split_axis=0, concat_axis=0, tiled=True
    )
    screened = pl.pallas_call(
        screen_kernel,
        out_shape=jax.ShapeDtypeStruct(couplings.shape, jnp.bfloat16),
        in_specs=[VMEM, VMEM],
        out_specs=pl.BlockSpec(memory_space=pl.ANY),
        scratch_shapes=[
            pltpu.VMEM(couplings.shape, jnp.bfloat16),
            pltpu.SemaphoreType.DMA((2,)),
        ],
        name="screen",
    )(onchip(factors), onchip(returned.reshape(energies * ROWS, LANES)))
    return screened.reshape(couplings.shape[0], 1, order, order)


def solution(mesh):
    placed = (
        P(None, ("wide", "sub"), None, None),
        P("pair", None, None),
        P("pair", None),
        P("pair"),
    )
    return jax.shard_map(
        per_device,
        mesh=mesh,
        in_specs=placed,
        out_specs=P("pair", ("wide", "sub"), None, None),
        check_vma=False,
    )
```

```python
import functools

import jax
import jax.numpy as jnp
from jax import lax
from jax.experimental import pallas as pl
from jax.experimental.pallas import tpu as pltpu
from jax.sharding import Mesh
from jax.sharding import PartitionSpec as P


LANES = 128
CHIPS_X = 4
ROWS = 8
VMEM = pl.BlockSpec(memory_space=pltpu.VMEM)
SMEM = pl.BlockSpec(memory_space=pltpu.SMEM)


def matmul(left, right):
    return jnp.dot(left, right, preferred_element_type=jnp.float32)


def matmul_t(left, right):
    return lax.dot_general(
        left, right, (((1,), (1,)), ((), ())), preferred_element_type=jnp.float32
    )


def pack(first, second):
    half = first.shape[0] // 2
    rest = jnp.concatenate(
        [
            first[:half, LANES:],
            first[half:, LANES:],
            second[:half, LANES:],
            second[half:, LANES:],
        ],
        axis=1,
    )
    return jnp.concatenate([first[:, :LANES], second[:, :LANES], rest], axis=0)


def unpack(packed, order, b):
    half = order // 2
    width = order - LANES
    rest = packed[2 * order : 2 * order + half, :]
    at = 2 * b * width
    tail = jnp.concatenate(
        [rest[:, at : at + width], rest[:, at + width : at + 2 * width]], axis=0
    )
    return jnp.concatenate([packed[b * order : (b + 1) * order, :], tail], axis=1)


def send_kernel(couplings, out):
    out[...] = pack(couplings[0], couplings[1])


def direct_kernel(blocks, partner, orbitals, couplings, out, factors, arriving, crossed):
    first = lax.rem(partner[0], 2)
    results = []
    for b in range(2):
        left = orbitals[blocks[b, 0]]
        right = orbitals[blocks[b, 1]]
        slot = first if b == 0 else 1 - first
        for side, factor in enumerate((left, right)):
            factors[2 * b + side] = factor
            arriving[2 * slot + side] = factor
        inner = matmul(left, couplings[b]).astype(jnp.bfloat16)
        results.append(matmul_t(inner, right))
    out[...] = pack(*results).astype(jnp.bfloat16)
    crossed[...] = jnp.full(crossed.shape, first, jnp.int32)


def mirror_kernel(factors, crossed, shifted, direct, out):
    results = []
    for b in range(2):
        coupling = unpack(shifted, factors.shape[1], b)
        across = matmul(factors[2 * b + 1], coupling).astype(jnp.bfloat16)
        results.append(matmul_t(factors[2 * b], across))
    arrived = pack(*results)
    order = factors.shape[1]
    swap = jnp.broadcast_to(crossed[0:1, :], arrived.shape) > 0
    half = (order - LANES) * 2
    rest = arrived[2 * order :]
    turned = jnp.concatenate(
        [
            arrived[order : 2 * order],
            arrived[:order],
            jnp.concatenate([rest[:, half:], rest[:, :half]], axis=1),
        ],
        axis=0,
    )
    mirror = jnp.where(swap, turned, arrived)
    used = direct.shape[0] // ROWS
    both = jnp.concatenate(
        [
            direct[...].astype(jnp.float32).reshape(used, ROWS, LANES),
            mirror.reshape(used, ROWS, LANES),
        ],
        axis=1,
    )
    out[:used] = both.astype(jnp.bfloat16)
    out[used:] = jnp.zeros((out.shape[0] - used, 2 * ROWS, LANES), jnp.bfloat16)


def convolve_kernel(tile, inner, incoming, out, first, second):
    count = incoming.shape[0]
    both = incoming[...].astype(jnp.float32)
    first[...] = both[:, :ROWS]
    second[...] = both[:, ROWS:]
    scale = count ** (-0.5)

    def slot(energy):
        return energy % inner * (count // inner) + energy // inner

    for e0 in range(0, count, tile):
        totals = [None] * tile
        for t0 in range(0, e0 + tile, tile):
            lhs = [first[slot(t0 + k)] for k in range(tile)]
            base = e0 - t0 - tile + 1
            rhs = [
                second[slot(base + k)] if base + k >= 0 else None
                for k in range(2 * tile - 1)
            ]
            for de in range(tile):
                for dt in range(tile):
                    other = rhs[de - dt + tile - 1]
                    if other is None:
                        continue
                    term = lhs[dt] * other
                    totals[de] = term if totals[de] is None else totals[de] + term
        for de in range(tile):
            total = (totals[de] * scale).astype(jnp.bfloat16)
            out[pl.ds(slot(e0 + de) * ROWS, ROWS), :] = total


def screen_kernel(factors, packed, out, held, sems):
    copies = []
    for b in range(2):
        polar = unpack(packed, held.shape[1], b)
        screened = matmul(factors[2 * b], polar).astype(jnp.bfloat16)
        held[b] = matmul_t(screened, factors[2 * b + 1]).astype(jnp.bfloat16)
        copy = pltpu.make_async_copy(held.at[b], out.at[b], sems.at[b])
        copy.start()
        copies.append(copy)
    for copy in copies:
        copy.wait()


def onchip(value):
    return pltpu.with_memory_space_constraint(value, pltpu.VMEM)


def per_device(orbitals, couplings, blocks, partner):
    axes = ("inside", "sub", "x")
    energies = lax.axis_size(axes)
    pairs = lax.axis_size("pair")
    order = couplings.shape[1]
    packed_rows = 2 * order * order // LANES
    packed = pltpu.VMEM((packed_rows, LANES), jnp.bfloat16)
    leaving = pl.pallas_call(
        send_kernel,
        out_shape=packed,
        in_specs=[VMEM],
        out_specs=VMEM,
        name="send",
    )(couplings)
    near = pairs // 2
    early = lax.axis_index("pair") < near
    from_late = lax.ppermute(leaving, "pair", [(i + near, i) for i in range(near)])
    from_early = lax.ppermute(leaving, "pair", [(i, i + near) for i in range(near)])
    sites = orbitals.reshape(orbitals.shape[0], order, order)
    chosen = pltpu.VMEM((4, order, order), jnp.bfloat16)
    direct, factors, arriving, crossed = pl.pallas_call(
        direct_kernel,
        out_shape=[packed, chosen, chosen, pltpu.VMEM((ROWS, LANES), jnp.int32)],
        in_specs=[SMEM, SMEM, VMEM, VMEM],
        out_specs=[VMEM] * 4,
        name="direct",
    )(blocks, partner, sites, couplings)
    result = pltpu.VMEM((energies * ROWS, LANES), jnp.bfloat16)

    def polarize(polar, shifted, direct, arriving, crossed):
        outgoing = pl.pallas_call(
            mirror_kernel,
            out_shape=pltpu.VMEM((energies, 2 * ROWS, LANES), jnp.bfloat16),
            in_specs=[VMEM] * 4,
            out_specs=VMEM,
            name="mirror",
        )(onchip(arriving), onchip(crossed), onchip(shifted), onchip(direct))
        incoming = lax.all_to_all(outgoing, axes, split_axis=0, concat_axis=0, tiled=True)
        return pl.pallas_call(
            functools.partial(convolve_kernel, 8, energies // lax.axis_size("x")),
            out_shape=result,
            in_specs=[VMEM],
            out_specs=VMEM,
            scratch_shapes=[pltpu.VMEM((energies, ROWS, LANES), jnp.float32)] * 2,
            name="convolve",
        )(onchip(incoming))

    def keep(polar, *_):
        return polar

    polar = jnp.zeros((energies * ROWS, LANES), jnp.bfloat16)
    polar = lax.cond(early, polarize, keep, polar, from_late, direct, arriving, crossed)
    polar = lax.cond(early, keep, polarize, polar, from_early, direct, arriving, crossed)
    returned = lax.all_to_all(
        polar.reshape(energies, ROWS, LANES), axes, split_axis=0, concat_axis=0, tiled=True
    )
    screened = pl.pallas_call(
        screen_kernel,
        out_shape=jax.ShapeDtypeStruct(couplings.shape, jnp.bfloat16),
        in_specs=[VMEM, VMEM],
        out_specs=pl.BlockSpec(memory_space=pl.ANY),
        scratch_shapes=[
            pltpu.VMEM(couplings.shape, jnp.bfloat16),
            pltpu.SemaphoreType.DMA((2,)),
        ],
        name="screen",
    )(onchip(factors), onchip(returned.reshape(energies * ROWS, LANES)))
    return screened.reshape(couplings.shape[0], 1, order, order)


def solution(mesh):
    sizes = mesh.shape
    split = Mesh(
        mesh.devices.reshape(CHIPS_X, -1, sizes["pair"], sizes["sub"]),
        ("x", "inside", "pair", "sub"),
    )
    energy = ("x", "inside", "sub")
    placed = (
        P(None, energy, None, None),
        P("pair", None, None),
        P("pair", None),
        P("pair"),
    )
    return jax.shard_map(
        per_device,
        mesh=split,
        in_specs=placed,
        out_specs=P("pair", energy, None, None),
        check_vma=False,
    )
```

```python
import functools

import jax
import jax.numpy as jnp
from jax import lax
from jax.experimental import pallas as pl
from jax.experimental.pallas import tpu as pltpu
from jax.sharding import Mesh
from jax.sharding import PartitionSpec as P


LANES = 128
CHIPS_X = 4
ROWS = 8
VMEM = pl.BlockSpec(memory_space=pltpu.VMEM)
SMEM = pl.BlockSpec(memory_space=pltpu.SMEM)


def matmul(left, right):
    return jnp.dot(left, right, preferred_element_type=jnp.float32)


def matmul_t(left, right):
    return lax.dot_general(
        left, right, (((1,), (1,)), ((), ())), preferred_element_type=jnp.float32
    )


def pack(first, second):
    half = first.shape[0] // 2
    rest = jnp.concatenate(
        [
            first[:half, LANES:],
            first[half:, LANES:],
            second[:half, LANES:],
            second[half:, LANES:],
        ],
        axis=1,
    )
    return jnp.concatenate([first[:, :LANES], second[:, :LANES], rest], axis=0)


def unpack(packed, order, b):
    half = order // 2
    width = order - LANES
    rest = packed[2 * order : 2 * order + half, :]
    at = 2 * b * width
    tail = jnp.concatenate(
        [rest[:, at : at + width], rest[:, at + width : at + 2 * width]], axis=0
    )
    return jnp.concatenate([packed[b * order : (b + 1) * order, :], tail], axis=1)


def send_kernel(couplings, out):
    out[...] = pack(couplings[0], couplings[1])


def direct_kernel(blocks, partner, orbitals, couplings, out, factors, arriving, crossed):
    first = lax.rem(partner[0], 2)
    results = []
    for b in range(2):
        left = orbitals[blocks[b, 0]]
        right = orbitals[blocks[b, 1]]
        slot = first if b == 0 else 1 - first
        for side, factor in enumerate((left, right)):
            factors[2 * b + side] = factor
            arriving[2 * slot + side] = factor
        inner = matmul(left, couplings[b]).astype(jnp.bfloat16)
        results.append(matmul_t(inner, right))
    out[...] = pack(*results).astype(jnp.bfloat16)
    crossed[...] = jnp.full(crossed.shape, first, jnp.int32)


def mirror_kernel(factors, crossed, shifted, direct, out):
    results = []
    for b in range(2):
        coupling = unpack(shifted, factors.shape[1], b)
        across = matmul(factors[2 * b + 1], coupling).astype(jnp.bfloat16)
        results.append(matmul_t(factors[2 * b], across))
    arrived = pack(*results)
    order = factors.shape[1]
    swap = jnp.broadcast_to(crossed[0:1, :], arrived.shape) > 0
    half = (order - LANES) * 2
    rest = arrived[2 * order :]
    turned = jnp.concatenate(
        [
            arrived[order : 2 * order],
            arrived[:order],
            jnp.concatenate([rest[:, half:], rest[:, :half]], axis=1),
        ],
        axis=0,
    )
    mirror = jnp.where(swap, turned, arrived)
    used = direct.shape[0] // ROWS
    both = jnp.concatenate(
        [
            direct[...].astype(jnp.float32).reshape(used, ROWS, LANES),
            mirror.reshape(used, ROWS, LANES),
        ],
        axis=1,
    )
    out[:used] = both.astype(jnp.bfloat16)
    out[used:] = jnp.zeros((out.shape[0] - used, 2 * ROWS, LANES), jnp.bfloat16)


def convolve_kernel(tile, inside, subs, incoming, out, first, second):
    count = incoming.shape[0]
    both = incoming[...].astype(jnp.float32)
    first[...] = both[:, :ROWS]
    second[...] = both[:, ROWS:]
    scale = count ** (-0.5)

    def slot(energy):
        rest, sub = divmod(energy, subs)
        x, place = divmod(rest, inside)
        return (place * (count // (inside * subs)) + x) * subs + sub

    for e0 in range(0, count, tile):
        totals = [None] * tile
        for t0 in range(0, e0 + tile, tile):
            lhs = [first[slot(t0 + k)] for k in range(tile)]
            base = e0 - t0 - tile + 1
            rhs = [
                second[slot(base + k)] if base + k >= 0 else None
                for k in range(2 * tile - 1)
            ]
            for de in range(tile):
                for dt in range(tile):
                    other = rhs[de - dt + tile - 1]
                    if other is None:
                        continue
                    term = lhs[dt] * other
                    totals[de] = term if totals[de] is None else totals[de] + term
        for de in range(0, tile, 2):
            pair = jnp.concatenate([totals[de], totals[de + 1]], axis=0) * scale
            out[pl.ds(slot(e0 + de) * ROWS, 2 * ROWS), :] = pair.astype(jnp.bfloat16)


def screen_kernel(factors, packed, out, held, sems):
    copies = []
    for b in range(2):
        polar = unpack(packed, held.shape[1], b)
        screened = matmul(factors[2 * b], polar).astype(jnp.bfloat16)
        held[b] = matmul_t(screened, factors[2 * b + 1]).astype(jnp.bfloat16)
        copy = pltpu.make_async_copy(held.at[b], out.at[b], sems.at[b])
        copy.start()
        copies.append(copy)
    for copy in copies:
        copy.wait()


def onchip(value):
    return pltpu.with_memory_space_constraint(value, pltpu.VMEM)


def per_device(orbitals, couplings, blocks, partner):
    axes = ("inside", "x", "sub")
    energies = lax.axis_size(axes)
    pairs = lax.axis_size("pair")
    order = couplings.shape[1]
    packed_rows = 2 * order * order // LANES
    packed = pltpu.VMEM((packed_rows, LANES), jnp.bfloat16)
    leaving = pl.pallas_call(
        send_kernel,
        out_shape=packed,
        in_specs=[VMEM],
        out_specs=VMEM,
        name="send",
    )(couplings)
    near = pairs // 2
    early = lax.axis_index("pair") < near
    from_late = lax.ppermute(leaving, "pair", [(i + near, i) for i in range(near)])
    from_early = lax.ppermute(leaving, "pair", [(i, i + near) for i in range(near)])
    sites = orbitals.reshape(orbitals.shape[0], order, order)
    chosen = pltpu.VMEM((4, order, order), jnp.bfloat16)
    direct, factors, arriving, crossed = pl.pallas_call(
        direct_kernel,
        out_shape=[packed, chosen, chosen, pltpu.VMEM((ROWS, LANES), jnp.int32)],
        in_specs=[SMEM, SMEM, VMEM, VMEM],
        out_specs=[VMEM] * 4,
        name="direct",
    )(blocks, partner, sites, couplings)
    result = pltpu.VMEM((energies * ROWS, LANES), jnp.bfloat16)

    def polarize(polar, shifted, direct, arriving, crossed):
        outgoing = pl.pallas_call(
            mirror_kernel,
            out_shape=pltpu.VMEM((energies, 2 * ROWS, LANES), jnp.bfloat16),
            in_specs=[VMEM] * 4,
            out_specs=VMEM,
            name="mirror",
        )(onchip(arriving), onchip(crossed), onchip(shifted), onchip(direct))
        incoming = lax.all_to_all(outgoing, axes, split_axis=0, concat_axis=0, tiled=True)
        return pl.pallas_call(
            functools.partial(
                convolve_kernel, 8, lax.axis_size("inside"), lax.axis_size("sub")
            ),
            out_shape=result,
            in_specs=[VMEM],
            out_specs=VMEM,
            scratch_shapes=[pltpu.VMEM((energies, ROWS, LANES), jnp.float32)] * 2,
            name="convolve",
        )(onchip(incoming))

    def keep(polar, *_):
        return polar

    polar = jnp.zeros((energies * ROWS, LANES), jnp.bfloat16)
    polar = lax.cond(early, polarize, keep, polar, from_late, direct, arriving, crossed)
    polar = lax.cond(early, keep, polarize, polar, from_early, direct, arriving, crossed)
    returned = lax.all_to_all(
        polar.reshape(energies, ROWS, LANES), axes, split_axis=0, concat_axis=0, tiled=True
    )
    screened = pl.pallas_call(
        screen_kernel,
        out_shape=jax.ShapeDtypeStruct(couplings.shape, jnp.bfloat16),
        in_specs=[VMEM, VMEM],
        out_specs=pl.BlockSpec(memory_space=pl.ANY),
        scratch_shapes=[
            pltpu.VMEM(couplings.shape, jnp.bfloat16),
            pltpu.SemaphoreType.DMA((2,)),
        ],
        name="screen",
    )(onchip(factors), onchip(returned.reshape(energies * ROWS, LANES)))
    return screened.reshape(couplings.shape[0], 1, order, order)


def solution(mesh):
    sizes = mesh.shape
    split = Mesh(
        mesh.devices.reshape(CHIPS_X, -1, sizes["pair"], sizes["sub"]),
        ("x", "inside", "pair", "sub"),
    )
    energy = ("x", "inside", "sub")
    placed = (
        P(None, energy, None, None),
        P("pair", None, None),
        P("pair", None),
        P("pair"),
    )
    return jax.shard_map(
        per_device,
        mesh=split,
        in_specs=placed,
        out_specs=P("pair", energy, None, None),
        check_vma=False,
    )
```
